128 devices in a mesh: stretch: 16 (over x, y), head: 8 (over z, core).
Axes of the slice: x: 4, y: 4, z: 4, core: 2. Of those that a mesh axis runs over, the one named last changes fastest.
Arguments:
- q_items: bfloat16 [16, 432, 32, 128], P('stretch', None, 'head'), may hold values from -6 to 6
- k_items: bfloat16 [16, 432, 8, 128], P('stretch', None, 'head'), may hold values from -6 to 6
- v_items: bfloat16 [16, 432, 8, 128], P('stretch', None, 'head'), may hold values from -6 to 6
- d_out: bfloat16 [16, 432, 32, 128], P('stretch', None, 'head'), may hold values from -6 to 6
- reader_query: float32 [2048, 32, 128], P('stretch', 'head'), may hold values from -6 to 6
- reader_span: int32 [2048], P('stretch'), may hold values from 1 to 16
- target: float32 [2048, 4096], P('stretch', 'head'), may hold values from -6 to 6
- out_proj: float32 [4096, 4096], P('stretch', 'head'), may hold values from -0.09375 to 0.09375
Outputs:
- q_items_grad: float32 [16, 432, 32, 128], P('stretch', None, 'head')
- k_items_grad: float32 [16, 432, 8, 128], P('stretch', None, 'head')
- v_items_grad: float32 [16, 432, 8, 128], P('stretch', None, 'head')
- reader_query_grad: float32 [2048, 32, 128], P('stretch', 'head')
- out_proj_grad: float32 [4096, 4096], P('stretch', 'head')
The draws below stay inside these ranges and needn't reach their ends.
All inputs are finite; a program needn't handle non-finite values.
Results may differ from the reference program's by a relative error of at most 0.0093.
Values may be sent and summed in bfloat16 or wider, within the bound.
No kernel may reach another device: no remote copies, remote signals or barrier semaphores. Data moves between devices by JAX's collectives and lax.ppermute only.
A program may use at most 128 MiB of HBM per device.

```python
import jax
import jax.numpy as jnp
from jax import lax

D = 4096
QUERY_HEADS = 32
KV_HEADS = 8
HEAD_DIM = 128
SEG_LEN = 384
BEACONS = 48
SEGMENTS = 16
READERS = 2048


def base_values(key, shape):
    return jnp.clip(jax.random.normal(key, shape, jnp.float32), -4.0, 4.0)


def draw_k_items(key, part):
    shape = (SEGMENTS, SEG_LEN + BEACONS, KV_HEADS, HEAD_DIM)
    drawn = base_values(jax.random.fold_in(key, 1), shape)
    return drawn.astype(jnp.bfloat16)


def draw_q_items(key, part):
    shape = (SEGMENTS, SEG_LEN + BEACONS, QUERY_HEADS, HEAD_DIM)
    drawn = base_values(jax.random.fold_in(key, 2), shape)
    return drawn.astype(jnp.bfloat16)


def draw_reader_query(key, part):
    shape = (READERS, QUERY_HEADS, HEAD_DIM)
    drawn = base_values(jax.random.fold_in(key, 3), shape)
    return drawn


def place_ends(values, stream_key, smallest, top_value):
    place = [jax.random.randint(jax.random.fold_in(stream_key, axis), (), 0, length) for axis, length in enumerate(values.shape)]
    longest = values.shape.index(max(values.shape))
    beside = place[:longest] + [(place[longest] + 1) % values.shape[longest]] + place[longest + 1:]
    return values.at[tuple(place)].set(smallest).at[tuple(beside)].set(top_value)


def levels(key, dims, shards, least, largest):
    loudness = 1.0
    for axis_at, shards_of in shards:
        heights = jax.random.uniform(jax.random.fold_in(jax.random.fold_in(key, 6), axis_at), (shards_of,), jnp.float32, least / len(shards), largest / len(shards))
        loudness = loudness * jnp.repeat(jnp.exp(heights), dims[axis_at] // shards_of).reshape((-1,) + (1,) * (len(dims) - 1 - axis_at))
    return loudness


def noise(own_key, extent, width, reach, split=(), kind=jnp.bfloat16):
    array = jax.random.normal(own_key, extent, jnp.float32) * width
    if len(split) > 0:
        array = levels(own_key, extent, split, -0.22, 0.18) * array
    return jnp.clip(array, min=-reach, max=reach).astype(kind)


def setup_inputs(seed: int = 0) -> dict:
    key_list = jax.random.split(jax.random.key(seed), 9)
    q_items = draw_q_items(jax.random.fold_in(key_list[8], 71), 0)
    k_items = draw_k_items(jax.random.fold_in(key_list[8], 71), 0)
    v_items = noise(key_list[2], (SEGMENTS, SEG_LEN + BEACONS, KV_HEADS, HEAD_DIM), 1.0, 6.0, ((0, 16), (2, 8)))
    d_out = noise(key_list[3], (SEGMENTS, SEG_LEN + BEACONS, QUERY_HEADS, HEAD_DIM), 1.0, 6.0, ((0, 16), (2, 8)))
    reader_query = draw_reader_query(jax.random.fold_in(key_list[8], 71), 0)
    reader_span = place_ends(jax.random.randint(key_list[5], (READERS,), 1, SEGMENTS + 1), jax.random.fold_in(key_list[5], 1), 1, SEGMENTS).astype(jnp.int32)
    target = noise(key_list[6], (READERS, D), 1.0, 6.0, ((0, 16), (1, 8)), jnp.float32)
    out_proj = noise(key_list[7], (D, D), D ** -0.5, 0.09375, ((0, 16), (1, 8)), jnp.float32)
    return {"q_items": q_items, "k_items": k_items, "v_items": v_items, "d_out": d_out, "reader_query": reader_query, "reader_span": reader_span, "target": target, "out_proj": out_proj}


def product(pattern, former, latter):
    return jnp.einsum(pattern, former.astype(jnp.float32), latter.astype(jnp.float32), precision=lax.Precision.HIGHEST)


def narrowed(values):
    return lax.optimization_barrier(values.astype(jnp.bfloat16))


def softmax_rows(scores, visible):
    masked = jnp.where(visible, scores, -1e30)
    row_top = jnp.max(masked, axis=-1, keepdims=True)
    raised = jnp.where(visible, jnp.exp(masked - row_top), 0.0)
    return raised / jnp.sum(raised, axis=-1, keepdims=True)


def segment_grads(block_index, q_block, k_block, v_block, d_block, beacon_k, beacon_v, key_block):
    item_count, query_heads, head_width = q_block.shape
    groups = k_block.shape[1]
    per_group = query_heads // groups
    scaling = head_width ** -0.5
    beacon_count = beacon_k.shape[0]
    all_keys = jnp.concatenate([beacon_k, k_block], axis=0)
    all_values = jnp.concatenate([beacon_v, v_block], axis=0)
    queries = q_block.reshape(item_count, groups, per_group, head_width)
    out_grads = d_block.reshape(item_count, groups, per_group, head_width)
    causal = jnp.arange(item_count)[:, None] >= jnp.arange(item_count)[None, :]
    earlier = jnp.broadcast_to((key_block < block_index)[None, :], (item_count, beacon_count))
    visible = jnp.concatenate([earlier, causal], axis=1)
    scores = product("sgah,kgh->gask", queries, all_keys) * scaling
    probs = softmax_rows(scores, visible)
    prob_grad = product("sgah,kgh->gask", out_grads, all_values)
    row_total = jnp.sum(probs * prob_grad, axis=-1, keepdims=True)
    score_grad = narrowed(probs * (prob_grad - row_total) * scaling)
    rounded = narrowed(probs)
    q_grad = product("gask,kgh->sgah", score_grad, all_keys).reshape(item_count, query_heads, head_width)
    k_grad = product("gask,sgah->kgh", score_grad, queries)
    v_grad = product("gask,sgah->kgh", rounded, out_grads)
    return q_grad, k_grad[beacon_count:], v_grad[beacon_count:], k_grad[:beacon_count], v_grad[:beacon_count]


def reference(q_items, k_items, v_items, d_out, reader_query, reader_span, target, out_proj):
    per_group = QUERY_HEADS // KV_HEADS
    scaling = HEAD_DIM ** -0.5
    beacon_total = SEGMENTS * BEACONS
    beacon_k = k_items[:, SEG_LEN:].reshape(beacon_total, KV_HEADS, HEAD_DIM)
    beacon_v = v_items[:, SEG_LEN:].reshape(beacon_total, KV_HEADS, HEAD_DIM)
    key_block = (jnp.arange(beacon_total) // BEACONS).astype(jnp.int32)

    def advance(carry, inputs):
        block_index, q_block, k_block, v_block, d_block = inputs
        q_grad, k_own, v_own, k_far, v_far = segment_grads(block_index, q_block, k_block, v_block, d_block, beacon_k, beacon_v, key_block)
        return (carry[0] + k_far, carry[1] + v_far), (q_grad, k_own, v_own)

    empty = jnp.zeros((beacon_total, KV_HEADS, HEAD_DIM), jnp.float32)
    (token_dk, token_dv), (q_grads, k_grads, v_grads) = lax.scan(
        advance, (empty, empty), (jnp.arange(SEGMENTS).astype(jnp.int32), q_items, k_items, v_items, d_out))

    wide_k = beacon_k.astype(jnp.float32)
    wide_v = beacon_v.astype(jnp.float32)
    queries = reader_query.reshape(READERS, KV_HEADS, per_group, HEAD_DIM)
    visible = key_block[None, :] < reader_span[:, None]
    scores = product("rgah,kgh->gark", queries, wide_k) * scaling
    probs = softmax_rows(scores, visible)
    attended = product("gark,kgh->rgah", probs, wide_v).reshape(READERS, D)
    errors = jnp.dot(attended, out_proj.T, precision=lax.Precision.HIGHEST) - target
    out_proj_grad = jnp.dot(errors.T, attended, precision=lax.Precision.HIGHEST)
    attended_grad = jnp.dot(errors, out_proj, precision=lax.Precision.HIGHEST).reshape(READERS, KV_HEADS, per_group, HEAD_DIM)
    prob_grad = product("rgah,kgh->gark", attended_grad, wide_v)
    row_total = jnp.sum(probs * prob_grad, axis=-1, keepdims=True)
    score_grad = probs * (prob_grad - row_total) * scaling
    reader_query_grad = product("gark,kgh->rgah", score_grad, wide_k).reshape(READERS, QUERY_HEADS, HEAD_DIM)
    reader_dk = product("gark,rgah->kgh", score_grad, queries)
    reader_dv = product("gark,rgah->kgh", probs, attended_grad)

    beacon_dk = (token_dk + reader_dk).reshape(SEGMENTS, BEACONS, KV_HEADS, HEAD_DIM)
    beacon_dv = (token_dv + reader_dv).reshape(SEGMENTS, BEACONS, KV_HEADS, HEAD_DIM)
    k_items_grad = k_grads.at[:, SEG_LEN:].add(beacon_dk)
    v_items_grad = v_grads.at[:, SEG_LEN:].add(beacon_dv)
    return q_grads, k_items_grad, v_items_grad, reader_query_grad, out_proj_grad
```

```python
import jax
import jax.numpy as jnp
from jax import lax
from jax.experimental import pallas as pl
from jax.experimental.pallas import tpu as pltpu
from jax.sharding import Mesh
from jax.sharding import PartitionSpec as P

SEG_LEN = 384
BEACONS = 48
ITEMS = SEG_LEN + BEACONS
SEGMENTS = 16
HEADS = 4
WIDTH = 128
KEYS = SEGMENTS * BEACONS
READERS = 128
FEATURES = HEADS * WIDTH
SIDE = 4
ROWS = SIDE * READERS
TILE = 896
PADDED = 2 * TILE
CHUNK = 192
SCALING = WIDTH ** (-0.5)
HIDDEN = -1e30
LIMIT = 48 * 1024 * 1024
STRETCH = ("x", "y")
HEAD = ("z", "core")

bf16 = jnp.bfloat16
f32 = jnp.float32


def nn(a, b):
    return lax.dot_general(a, b, (((1,), (0,)), ((), ())), preferred_element_type=f32)


def nt(a, b):
    return lax.dot_general(a, b, (((1,), (1,)), ((), ())), preferred_element_type=f32)


def tn(a, b):
    return lax.dot_general(a, b, (((0,), (0,)), ((), ())), preferred_element_type=f32)


def halves(value):
    high = value.astype(bf16)
    return high, (value - high.astype(f32)).astype(bf16)


def shifted(value, axis, by):
    size = lax.axis_size(axis)
    return lax.ppermute(value, axis, [(i, (i + by) % size) for i in range(size)])


def whole(shape, dtype):
    return jax.ShapeDtypeStruct(shape, dtype)


def kernel_call(kernel, outs, scratch=(), flops=0, moved=0, scalars=True, inputs=1):
    vmem = pl.BlockSpec(memory_space=pltpu.VMEM)
    first = [pl.BlockSpec(memory_space=pltpu.SMEM)] if scalars else []
    return pl.pallas_call(
        kernel,
        out_shape=outs,
        in_specs=first + [vmem] * inputs,
        out_specs=jax.tree.map(lambda _: vmem, outs),
        scratch_shapes=list(scratch),
        compiler_params=pltpu.CompilerParams(vmem_limit_bytes=LIMIT),
        cost_estimate=pl.CostEstimate(flops=flops, transcendentals=0, bytes_accessed=moved),
    )


def segment_kernel(place, q, d, far_kv, own_kv, dq, far, own, score, grad):
    seen_beacons = place[0] * BEACONS

    for t in range(2):
        rows = pl.ds(t * TILE, TILE)
        own_chunks = [(0, 224)] if t == 0 else [(0, 224), (224, 208)]
        q_t = q[rows, :]
        d_t = d[rows, :]

        def far_scores(i, top):
            at = pl.multiple_of(i * CHUNK, CHUNK)
            s = nt(far_kv[pl.ds(at, CHUNK), :WIDTH], q_t) * SCALING
            key = lax.broadcasted_iota(jnp.int32, s.shape, 0) + at
            s = jnp.where(key < seen_beacons, s, HIDDEN)
            score[pl.ds(at, CHUNK), :] = s
            return jnp.maximum(top, jnp.max(s, axis=0, keepdims=True))

        top = jnp.full((1, TILE), HIDDEN, f32)
        top = lax.fori_loop(0, KEYS // CHUNK, far_scores, top)
        for at, count in own_chunks:
            s = nt(own_kv[pl.ds(at, count), :WIDTH], q_t) * SCALING
            key = lax.broadcasted_iota(jnp.int32, s.shape, 0) + at
            item = (lax.broadcasted_iota(jnp.int32, s.shape, 1) + t * TILE) >> 2
            s = jnp.where(key <= item, s, HIDDEN)
            score[pl.ds(KEYS + at, count), :] = s
            top = jnp.maximum(top, jnp.max(s, axis=0, keepdims=True))

        def raised(at, count, v, sums):
            e = jnp.exp(score[pl.ds(at, count), :] - top)
            g = nt(v, d_t)
            score[pl.ds(at, count), :] = e
            grad[pl.ds(at, count), :] = g
            return (
                sums[0] + jnp.sum(e, axis=0, keepdims=True),
                sums[1] + jnp.sum(e * g, axis=0, keepdims=True),
            )

        def far_raised(i, sums):
            at = pl.multiple_of(i * CHUNK, CHUNK)
            return raised(at, CHUNK, far_kv[pl.ds(at, CHUNK), WIDTH:], sums)

        sums = (jnp.zeros((1, TILE), f32), jnp.zeros((1, TILE), f32))
        sums = lax.fori_loop(0, KEYS // CHUNK, far_raised, sums)
        for at, count in own_chunks:
            sums = raised(KEYS + at, count, own_kv[pl.ds(at, count), WIDTH:], sums)
        inverse = 1.0 / sums[0]
        total = sums[1] * inverse

        def grads(at, count, k):
            p = score[pl.ds(at, count), :] * inverse
            ds = (p * (grad[pl.ds(at, count), :] - total) * SCALING).astype(bf16)
            return nn(ds, q_t), nn(p.astype(bf16), d_t), tn(k, ds)

        def far_grads(i, acc):
            at = pl.multiple_of(i * CHUNK, CHUNK)
            dk, dv, part = grads(at, CHUNK, far_kv[pl.ds(at, CHUNK), :WIDTH])
            if t == 0:
                far[pl.ds(at, CHUNK), :WIDTH] = dk
                far[pl.ds(at, CHUNK), WIDTH:] = dv
            else:
                far[pl.ds(at, CHUNK), :WIDTH] += dk
                far[pl.ds(at, CHUNK), WIDTH:] += dv
            return acc + part

        acc = lax.fori_loop(0, KEYS // CHUNK, far_grads, jnp.zeros((WIDTH, TILE), f32))
        for at, count in own_chunks:
            dk, dv, part = grads(KEYS + at, count, own_kv[pl.ds(at, count), :WIDTH])
            acc = acc + part
            if t == 1 and at == 0:
                own[pl.ds(at, count), :WIDTH] += dk
                own[pl.ds(at, count), WIDTH:] += dv
            else:
                own[pl.ds(at, count), :WIDTH] = dk
                own[pl.ds(at, count), WIDTH:] = dv
        dq[rows, :] = acc.T


def reader_kernel(seen, q, kv, probs, attended):
    k = kv[:, :WIDTH]
    v = kv[:, WIDTH:]
    for h in range(0, HEADS, 2):
        cols = pl.ds(h * READERS, 2 * READERS)
        q_all = q[cols, :]
        q_0 = q_all.astype(bf16)
        q_1, q_2 = halves(q_all - q_0.astype(f32))
        s = (nt(k, q_0) + nt(k, q_1) + nt(k, q_2)) * SCALING
        key = lax.broadcasted_iota(jnp.int32, s.shape, 0)
        s = jnp.where(key < seen[:, cols], s, HIDDEN)
        e = jnp.exp(s - jnp.max(s, axis=0, keepdims=True))
        p = e * (1.0 / jnp.sum(e, axis=0, keepdims=True))
        probs[:, cols] = p
        high, low = halves(p)
        out = tn(v, high) + tn(v, low)
        for i in range(2):
            at = (h + i) * WIDTH
            attended[:, at : at + WIDTH] = out[:, i * READERS : (i + 1) * READERS].T.astype(bf16)


def reader_grad_kernel(g_0, g_1, g_2, g_3, probs, q, kv, far, dq, beacon_grad):
    k = kv[:, :WIDTH]
    v = kv[:, WIDTH:]
    dk = far[:, :WIDTH]
    dv = far[:, WIDTH:]
    for h in range(0, HEADS, 2):
        cols = pl.ds(h * READERS, 2 * READERS)
        g = []
        for i in range(2):
            at = slice((h + i) * WIDTH, (h + i + 1) * WIDTH)
            g.append(
                g_0[:, at] + g_1[:, at].astype(f32) + g_2[:, at].astype(f32) + g_3[:, at].astype(f32)
            )
        high, low = halves(jnp.concatenate(g, axis=0))
        p = probs[:, cols]
        pg = nt(v, high) + nt(v, low)
        total = jnp.sum(p * pg, axis=0, keepdims=True)
        ds_high, ds_low = halves(p * (pg - total) * SCALING)
        out = tn(k, ds_high) + tn(k, ds_low)
        for i in range(2):
            dq[:, h + i, :] = out[:, i * READERS : (i + 1) * READERS].T
        dk = dk + nn(ds_high, q[cols, :].astype(bf16))
        dv = dv + nn(p.astype(bf16), high)
    beacon_grad[:, :WIDTH] = dk.astype(bf16)
    beacon_grad[:, WIDTH:] = dv.astype(bf16)


def predict_kernel(place, a_0, a_1, a_2, a_3, w, own, other):
    z = place[1]
    core = place[2]
    a = jnp.concatenate([a_0[...], a_1[...], a_2[...], a_3[...]], axis=0)
    for i in range(SIDE):
        at = lax.rem(z + i, SIDE)
        other[i] = nt(a, w[at, 1 - core]).astype(bf16)
        own[i] = nt(a, w[at, core])


def gather_errors(place, mine, others, errors):
    z = place[1]
    core = place[2]
    for i in range(SIDE):
        at = lax.rem(z + SIDE - i, SIDE)
        errors[at, core] = mine[i][...]
        errors[at, 1 - core] = others[i][...]


def attended_grad_kernel(place, e_0, e_1, e_2, e_3, o_0, o_1, o_2, o_3, w, g_0, g_1, g_2, g_3, errors):
    gather_errors(place, (e_0, e_1, e_2, e_3), (o_0, o_1, o_2, o_3), errors)
    for i, out in enumerate((g_0, g_1, g_2, g_3)):
        rows = pl.ds(i * READERS, READERS)
        acc = jnp.zeros((READERS, FEATURES), f32)
        for b in range(SIDE):
            e = jnp.concatenate([errors[b, 0, rows, :], errors[b, 1, rows, :]], axis=1)
            acc = acc + nn(e, jnp.concatenate([w[b, 0], w[b, 1]], axis=0))
        out[...] = acc.astype(out.dtype)


def projection_grad_kernel(
    place, e_0, e_1, e_2, e_3, o_0, o_1, o_2, o_3, a_0, a_1, a_2, a_3, p_0, p_1, p_2, p_3, errors
):
    gather_errors(place, (e_0, e_1, e_2, e_3), (o_0, o_1, o_2, o_3), errors)
    x = place[3]
    a = jnp.concatenate([a_0[...], a_1[...], a_2[...], a_3[...]], axis=0)
    for i, out in enumerate((p_0, p_1, p_2, p_3)):
        at = lax.rem(x + i, SIDE)
        for half in range(2):
            out[half * WIDTH : (half + 1) * WIDTH, :] = tn(errors[at, half], a).astype(bf16)


def body(q_items, k_items, v_items, d_out, reader_query, reader_span, target, out_proj):
    x = lax.axis_index("x")
    y = lax.axis_index("y")
    z = lax.axis_index("z")
    core = lax.axis_index("core")
    place = jnp.stack([x * SIDE + y, z, core, x]).astype(jnp.int32)

    w_all = lax.all_gather(out_proj.astype(bf16), "x", axis=0, tiled=True)
    w_all = w_all.reshape(SIDE, 2, WIDTH, FEATURES)

    own_kv = jnp.concatenate(
        [k_items.reshape(ITEMS, WIDTH), v_items.reshape(ITEMS, WIDTH)], axis=1
    )
    sent = jnp.broadcast_to(own_kv[None, SEG_LEN:], (SEGMENTS, BEACONS, 2 * WIDTH))
    far_kv = lax.all_to_all(sent, STRETCH, 0, 0, tiled=True).reshape(KEYS, 2 * WIDTH)

    parts = target.reshape(READERS, 2, 2, WIDTH).transpose(2, 1, 0, 3)
    kept = lax.dynamic_index_in_dim(parts, core, 0, keepdims=False)
    swapped = lax.ppermute(
        lax.dynamic_index_in_dim(parts, 1 - core, 0, keepdims=False), "core", [(0, 1), (1, 0)]
    )
    by_y = jnp.concatenate(
        [jnp.where(core == 0, kept, swapped), jnp.where(core == 0, swapped, kept)], axis=0
    )
    targets = [
        lax.dynamic_index_in_dim(by_y, lax.rem(y + i, SIDE), 0, keepdims=False) for i in range(SIDE)
    ]
    targets = [targets[0]] + [shifted(targets[i], "y", i) for i in range(1, SIDE)]

    rq = reader_query.transpose(1, 0, 2).reshape(HEADS * READERS, WIDTH)
    seen = jnp.tile(reader_span * BEACONS, HEADS)[None, :]
    probs, attended = kernel_call(
        reader_kernel,
        (whole((KEYS, HEADS * READERS), f32), whole((READERS, FEATURES), bf16)),
        scalars=False,
        inputs=3,
        flops=5 * 2 * KEYS * HEADS * READERS * WIDTH,
        moved=3 * 1024 * 1024,
    )(seen, rq, far_kv)

    a = [attended] + [shifted(attended, "y", i) for i in range(1, SIDE)]

    pad = ((0, PADDED - ITEMS * HEADS), (0, 0))
    q_rows = jnp.pad(q_items.reshape(ITEMS * HEADS, WIDTH), pad)
    d_rows = jnp.pad(d_out.reshape(ITEMS * HEADS, WIDTH), pad)
    dq_rows, far_grad, own_grad = kernel_call(
        segment_kernel,
        (
            whole((PADDED, WIDTH), f32),
            whole((KEYS, 2 * WIDTH), f32),
            whole((ITEMS, 2 * WIDTH), f32),
        ),
        scratch=(
            pltpu.VMEM((KEYS + ITEMS, TILE), f32),
            pltpu.VMEM((KEYS + ITEMS, TILE), f32),
        ),
        inputs=4,
        flops=5 * 2 * (KEYS + ITEMS) * PADDED * WIDTH,
        moved=4 * 1024 * 1024,
    )(place, q_rows, d_rows, far_kv, own_kv)

    own, other = kernel_call(
        predict_kernel,
        (whole((SIDE, ROWS, WIDTH), f32), whole((SIDE, ROWS, WIDTH), bf16)),
        inputs=5,
        flops=2 * ROWS * FEATURES * 1024,
        moved=3 * 1024 * 1024,
    )(place, *a, w_all)
    from_core = lax.ppermute(other, "core", [(0, 1), (1, 0)])
    chip = own + from_core.astype(f32)
    arrived = [shifted(chip[i].astype(bf16), "z", i) for i in range(1, SIDE)]
    total = chip[0] - jnp.concatenate(targets, axis=0)
    for part in arrived:
        total = total + part.astype(f32)
    error = total.astype(bf16)

    mine = [error] + [shifted(error, "z", i) for i in range(1, SIDE)]
    others = [lax.ppermute(e, "core", [(0, 1), (1, 0)]) for e in mine]
    stack = pltpu.VMEM((SIDE, 2, ROWS, WIDTH), bf16)
    piece = (READERS, FEATURES)
    g = kernel_call(
        attended_grad_kernel,
        (whole(piece, f32), whole(piece, bf16), whole(piece, bf16), whole(piece, bf16)),
        scratch=(stack,),
        inputs=9,
        flops=2 * ROWS * FEATURES * 1024,
        moved=3 * 1024 * 1024,
    )(place, *mine, *others, w_all)
    g = [g[0]] + [shifted(g[i], "y", -i) for i in range(1, SIDE)]

    block = whole((2 * WIDTH, FEATURES), bf16)
    w_grad = kernel_call(
        projection_grad_kernel,
        (block,) * SIDE,
        scratch=(stack,),
        inputs=12,
        flops=2 * ROWS * FEATURES * 1024,
        moved=3 * 1024 * 1024,
    )(place, *mine, *others, *a)
    out_proj_grad = w_grad[0].astype(f32)
    for i in range(1, SIDE):
        out_proj_grad = out_proj_grad + shifted(w_grad[i], "x", i).astype(f32)

    reader_query_grad, beacon_grad = kernel_call(
        reader_grad_kernel,
        (whole((READERS, HEADS, WIDTH), f32), whole((KEYS, 2 * WIDTH), bf16)),
        scalars=False,
        inputs=8,
        flops=8 * 2 * KEYS * HEADS * READERS * WIDTH,
        moved=5 * 1024 * 1024,
    )(*g, probs, rq, far_kv, far_grad)

    pieces = beacon_grad.reshape(SEGMENTS, BEACONS, 2 * WIDTH)
    owned = lax.all_to_all(pieces, STRETCH, 0, 0, tiled=True).astype(f32).sum(axis=0)
    own_grad = own_grad.at[SEG_LEN:].add(owned)
    q_items_grad = dq_rows[: ITEMS * HEADS].reshape(1, ITEMS, HEADS, WIDTH)
    k_items_grad = own_grad[:, :WIDTH].reshape(1, ITEMS, 1, WIDTH)
    v_items_grad = own_grad[:, WIDTH:].reshape(1, ITEMS, 1, WIDTH)
    return q_items_grad, k_items_grad, v_items_grad, reader_query_grad, out_proj_grad


def solution(mesh):
    axes = Mesh(mesh.devices.reshape(SIDE, SIDE, SIDE, 2), STRETCH + HEAD)
    items = P(STRETCH, None, HEAD, None)
    return jax.shard_map(
        body,
        mesh=axes,
        in_specs=(
            items,
            items,
            items,
            items,
            P(STRETCH, HEAD, None),
            P(STRETCH),
            P(STRETCH, HEAD),
            P(STRETCH, HEAD),
        ),
        out_specs=(items, items, items, P(STRETCH, HEAD, None), P(STRETCH, HEAD)),
        check_vma=False,
    )
```

```python
import jax
import jax.numpy as jnp
from jax import lax
from jax.experimental import pallas as pl
from jax.experimental.pallas import tpu as pltpu
from jax.sharding import Mesh
from jax.sharding import PartitionSpec as P

SEG_LEN = 384
BEACONS = 48
ITEMS = SEG_LEN + BEACONS
SEGMENTS = 16
HEADS = 4
WIDTH = 128
KEYS = SEGMENTS * BEACONS
READERS = 128
FEATURES = HEADS * WIDTH
SIDE = 4
ROWS = SIDE * READERS
PADDED = 1792
PARTS = ((0, 512), (512, 512), (1024, 384), (1408, 384))
CHUNK = 192
SCALING = WIDTH ** (-0.5)
HIDDEN = -1e30
EXPONENT = SCALING * 1.4426950408889634
CORES = [(0, 1), (1, 0)]
STRETCH = ("x", "y")
HEAD = ("z", "core")

bf16 = jnp.bfloat16
f32 = jnp.float32


def nn(a, b):
    return lax.dot_general(a, b, (((1,), (0,)), ((), ())), preferred_element_type=f32)


def nt(a, b):
    return lax.dot_general(a, b, (((1,), (1,)), ((), ())), preferred_element_type=f32)


def tn(a, b):
    return lax.dot_general(a, b, (((0,), (0,)), ((), ())), preferred_element_type=f32)


def halves(value):
    high = value.astype(bf16)
    return high, (value - high.astype(f32)).astype(bf16)


def shifted(value, axis, by):
    size = lax.axis_size(axis)
    return lax.ppermute(value, axis, [(i, (i + by) % size) for i in range(size)])


VMEM = pl.BlockSpec(memory_space=pltpu.VMEM)
HBM = pl.BlockSpec(memory_space=pltpu.HBM)
SMEM = pl.BlockSpec(memory_space=pltpu.SMEM)


def kernel_call(kernel, ins, outs, scratch=(), limit=16, flops=0, moved=0, aliases={}):
    return pl.pallas_call(
        kernel,
        out_shape=tuple(jax.ShapeDtypeStruct(shape, dtype) for shape, dtype, _ in outs),
        in_specs=list(ins),
        out_specs=tuple(spec for _, _, spec in outs),
        scratch_shapes=list(scratch),
        input_output_aliases=aliases,
        compiler_params=pltpu.CompilerParams(vmem_limit_bytes=limit * 1024 * 1024),
        cost_estimate=pl.CostEstimate(flops=flops, transcendentals=0, bytes_accessed=moved),
    )


def turned(index):
    return lax.rem(index + 2 * SIDE, SIDE)


def segment_kernel(start, count, first):
    own_keys = min((start + count) // HEADS, ITEMS)
    kept = min(count, ITEMS * HEADS - start)
    chunks = [(at, CHUNK) for at in range(0, KEYS, CHUNK)] + [(KEYS, own_keys)]

    def kernel(place, q, d, far_kv, own_kv, *refs):
        dq, far, own, score, grad, dq_rows, done = refs[-7:]
        rows = pl.ds(start, count)
        q_t = q[rows, :]
        d_t = d[rows, :]

        def keys(at, n):
            return far_kv[at : at + n, :WIDTH] if at < KEYS else own_kv[:n, :WIDTH]

        def values(at, n):
            return far_kv[at : at + n, WIDTH:] if at < KEYS else own_kv[:n, WIDTH:]

        top = jnp.full((1, count), HIDDEN, f32)
        for at, n in chunks:
            s = nt(keys(at, n), q_t)
            key = lax.broadcasted_iota(jnp.int32, s.shape, 0)
            if at < KEYS:
                s = jnp.where(key < place[0] * BEACONS - at, s, HIDDEN)
            else:
                item = (lax.broadcasted_iota(jnp.int32, s.shape, 1) + start) >> 2
                s = jnp.where(key <= item, s, HIDDEN)
            score[at : at + n, :] = s
            grad[at : at + n, :] = nt(values(at, n), d_t)
            top = jnp.maximum(top, jnp.max(s, axis=0, keepdims=True))

        bottom = jnp.zeros((1, count), f32)
        total = jnp.zeros((1, count), f32)
        for at, n in chunks:
            e = jnp.exp2((score[at : at + n, :] - top) * EXPONENT)
            score[at : at + n, :] = e
            bottom = bottom + jnp.sum(e, axis=0, keepdims=True)
            total = total + jnp.sum(e * grad[at : at + n, :], axis=0, keepdims=True)
        inverse = 1.0 / bottom
        total = total * inverse

        acc = jnp.zeros((WIDTH, count), f32)
        for at, n in chunks:
            p = score[at : at + n, :] * inverse
            ds = (p * (grad[at : at + n, :] - total)).astype(bf16)
            dk = nn(ds, q_t) * SCALING
            dv = nn(p.astype(bf16), d_t)
            acc = acc + tn(keys(at, n), ds)
            out = far.at[at : at + n] if at < KEYS else own.at[:n]
            if first:
                out[:, :WIDTH] = dk
                out[:, WIDTH:] = dv
            else:
                out[:, :WIDTH] += dk
                out[:, WIDTH:] += dv
        if first:
            own[own_keys:, :] = jnp.zeros((ITEMS - own_keys, 2 * WIDTH), f32)
        dq_rows[...] = (acc * SCALING).T
        copy = pltpu.make_async_copy(
            dq_rows.at[pl.ds(0, kept)], dq.at[pl.ds(start, kept)], done
        )
        copy.start()
        copy.wait()

    return kernel


def target_kernel(place, target, keep, send):
    left = place[2] == 0
    for b in range(2):
        first = target[:, 2 * b * WIDTH : (2 * b + 1) * WIDTH]
        second = target[:, (2 * b + 1) * WIDTH : (2 * b + 2) * WIDTH]
        keep[b] = jnp.where(left, first, second)
        send[b] = jnp.where(left, second, first)


def reader_kernel(place, seen, q, kv, keep, got, probs, a_0, a_1, a_2, a_3, p_scr, done):
    k = kv[:, :WIDTH]
    v = kv[:, WIDTH:]
    outs = (a_0, a_1, a_2, a_3)
    copies = []
    for h in range(0, HEADS, 2):
        cols = pl.ds(h * READERS, 2 * READERS)
        q_all = q[cols, :]
        q_0 = q_all.astype(bf16)
        q_1, q_2 = halves(q_all - q_0.astype(f32))
        s = nt(k, q_0) + nt(k, q_1) + nt(k, q_2)
        key = lax.broadcasted_iota(jnp.int32, s.shape, 0)
        s = jnp.where(key < seen[:, cols], s, HIDDEN)
        e = jnp.exp2((s - jnp.max(s, axis=0, keepdims=True)) * EXPONENT)
        p = e * (1.0 / jnp.sum(e, axis=0, keepdims=True))
        p_scr[h // 2] = p
        copies.append(pltpu.make_async_copy(p_scr.at[h // 2], probs.at[h // 2], done.at[h // 2]))
        copies[-1].start()
        high, low = halves(p)
        out = tn(v, high) + tn(v, low)
        for i in range(2):
            at = (h + i) * WIDTH
            part = out[:, i * READERS : (i + 1) * READERS].T.astype(bf16)
            for a in outs:
                a[:, at : at + WIDTH] = part
    for i, a in enumerate(outs):
        side = lax.rem(place[4] + i, SIDE)
        here = (side >> 1) == place[2]
        t = jnp.where(here, keep[side & 1], got[side & 1])
        high, low = halves(t)
        a[:, FEATURES : FEATURES + WIDTH] = high
        a[:, FEATURES + WIDTH :] = low
    for copy in copies:
        copy.wait()


def beacon_grad_kernel(g_0, g_1, g_2, g_3, probs, q, kv, far, score_grad, beacon_grad, p_scr, done):
    copies = [
        pltpu.make_async_copy(probs.at[i], p_scr.at[i], done.at[i]) for i in range(HEADS // 2)
    ]
    for copy in copies:
        copy.start()
    v = kv[:, WIDTH:]
    dk = jnp.zeros((KEYS, WIDTH), f32)
    dv = far[:, WIDTH:]
    for h in range(0, HEADS, 2):
        cols = pl.ds(h * READERS, 2 * READERS)
        g = []
        for i in range(2):
            at = slice((h + i) * WIDTH, (h + i + 1) * WIDTH)
            g.append(
                g_0[:, at] + g_1[:, at].astype(f32) + g_2[:, at].astype(f32) + g_3[:, at].astype(f32)
            )
        high, low = halves(jnp.concatenate(g, axis=0))
        pg = nt(v, high) + nt(v, low)
        copies[h // 2].wait()
        p = p_scr[h // 2]
        total = jnp.sum(p * pg, axis=0, keepdims=True)
        ds = (p * (pg - total)).astype(bf16)
        score_grad[:, cols] = ds
        dk = dk + nn(ds, q[cols, :].astype(bf16))
        dv = dv + nn(p.astype(bf16), high)
    beacon_grad[:, :WIDTH] = (far[:, :WIDTH] + dk * SCALING).astype(bf16)
    beacon_grad[:, WIDTH:] = dv.astype(bf16)


def query_grad_kernel(score_grad, kv, dq):
    out = tn(kv[:, :WIDTH], score_grad[...]) * SCALING
    for h in range(HEADS):
        dq[:, h, :] = out[:, h * READERS : (h + 1) * READERS].T


def predict_kernel(
    place, a_0, a_1, a_2, a_3, w_0, w_1, w_2, w_3, o_0, o_1, o_2, o_3, other, a_out, w_out, a_scr, w_scr, done
):
    z = place[1]
    left = place[2] == 0
    for i, a in enumerate((a_0, a_1, a_2, a_3)):
        a_scr[i * READERS : (i + 1) * READERS, :] = a[:, :FEATURES]
    for i, w in enumerate((w_0, w_1, w_2, w_3)):
        w_scr[turned(place[3] - i)] = w[...]
    copies = [
        pltpu.make_async_copy(a_scr, a_out, done.at[0]),
        pltpu.make_async_copy(w_scr, w_out, done.at[1]),
    ]
    for copy in copies:
        copy.start()
    for i, own in enumerate((o_0, o_1, o_2, o_3)):
        both = nt(a_scr[...], w_scr[turned(z + i)])
        mine = jnp.where(left, both[:, :WIDTH], both[:, WIDTH:])
        other[i] = jnp.where(left, both[:, WIDTH:], both[:, :WIDTH]).astype(bf16)
        if i == 0:
            for j, a in enumerate((a_0, a_1, a_2, a_3)):
                rows = slice(j * READERS, (j + 1) * READERS)
                high = a[:, FEATURES : FEATURES + WIDTH].astype(f32)
                own[rows, :] = mine[rows] - (high + a[:, FEATURES + WIDTH :].astype(f32))
        else:
            own[...] = mine
    for copy in copies:
        copy.wait()


def chip_sum_kernel(o_0, o_1, o_2, o_3, other, base, c_1, c_2, c_3):
    base[...] = o_0[...] + other[0].astype(f32)
    c_1[...] = (o_1[...] + other[1].astype(f32)).astype(bf16)
    c_2[...] = (o_2[...] + other[2].astype(f32)).astype(bf16)
    c_3[...] = (o_3[...] + other[3].astype(f32)).astype(bf16)


def gather_errors(place, mine, others, errors):
    z = place[1]
    left = place[2] == 0
    for i in range(SIDE):
        at = turned(z - i)
        e = mine[i][...]
        o = others[i][...]
        errors[at, :, :WIDTH] = jnp.where(left, e, o)
        errors[at, :, WIDTH:] = jnp.where(left, o, e)


def attended_grad_kernel(
    place, e_0, e_1, e_2, e_3, o_0, o_1, o_2, o_3, w, g_0, g_1, g_2, g_3, errors, w_scr, done
):
    copy = pltpu.make_async_copy(w, w_scr, done)
    copy.start()
    gather_errors(place, (e_0, e_1, e_2, e_3), (o_0, o_1, o_2, o_3), errors)
    copy.wait()
    for i, out in enumerate((g_0, g_1, g_2, g_3)):
        acc = jnp.zeros((READERS, FEATURES), f32)
        for b in range(SIDE):
            acc = acc + nn(errors[b, i * READERS : (i + 1) * READERS, :], w_scr[b])
        out[...] = acc.astype(out.dtype)


def projection_grad_kernel(
    place, e_0, e_1, e_2, e_3, o_0, o_1, o_2, o_3, a, p_0, p_1, p_2, p_3, errors, a_scr, done
):
    copy = pltpu.make_async_copy(a, a_scr, done)
    copy.start()
    gather_errors(place, (e_0, e_1, e_2, e_3), (o_0, o_1, o_2, o_3), errors)
    copy.wait()
    for i, out in enumerate((p_0, p_1, p_2, p_3)):
        out[...] = tn(errors[turned(place[3] + i)], a_scr[...]).astype(out.dtype)


def items_grad_kernel(own, owned, dk, dv):
    total = jnp.sum(owned[...].astype(f32), axis=0)
    dk[:SEG_LEN, :] = own[:SEG_LEN, :WIDTH]
    dv[:SEG_LEN, :] = own[:SEG_LEN, WIDTH:]
    dk[SEG_LEN:, :] = own[SEG_LEN:, :WIDTH] + total[:, :WIDTH]
    dv[SEG_LEN:, :] = own[SEG_LEN:, WIDTH:] + total[:, WIDTH:]


def body(q_items, k_items, v_items, d_out, reader_query, reader_span, target, out_proj):
    x = lax.axis_index("x")
    y = lax.axis_index("y")
    z = lax.axis_index("z")
    core = lax.axis_index("core")
    place = jnp.stack([x * SIDE + y, z, core, x, y]).astype(jnp.int32)
    together = lax.optimization_barrier
    sems = pltpu.SemaphoreType.DMA
    product = 2 * ROWS * FEATURES * 1024
    reader_product = 2 * KEYS * HEADS * READERS * WIDTH
    megabyte = 1024 * 1024

    own_kv = jnp.concatenate(
        [k_items.reshape(ITEMS, WIDTH), v_items.reshape(ITEMS, WIDTH)], axis=1
    )
    sent = jnp.broadcast_to(own_kv[None, SEG_LEN:], (SEGMENTS, BEACONS, 2 * WIDTH))
    far_kv = lax.all_to_all(sent, STRETCH, 0, 0, tiled=True).reshape(KEYS, 2 * WIDTH)

    w = out_proj.astype(bf16)
    w = [w] + [shifted(w, "x", i) for i in range(1, SIDE)]

    keep, send = kernel_call(
        target_kernel,
        [SMEM, VMEM],
        [((2, READERS, WIDTH), f32, VMEM)] * 2,
        moved=megabyte // 2,
    )(place, target)
    got = lax.ppermute(send, "core", CORES)

    pad = ((0, PADDED - ITEMS * HEADS), (0, 0))
    q_rows = jnp.pad(q_items.reshape(ITEMS * HEADS, WIDTH), pad)
    d_rows = jnp.pad(d_out.reshape(ITEMS * HEADS, WIDTH), pad)
    rq = reader_query.transpose(1, 0, 2).reshape(HEADS * READERS, WIDTH)
    seen = jnp.tile(reader_span * BEACONS, HEADS)[None, :]

    far_kv, keep, got, w, q_rows, d_rows, rq, seen = together(
        (far_kv, keep, got, w, q_rows, d_rows, rq, seen)
    )

    probs, *a = kernel_call(
        reader_kernel,
        [SMEM] + [VMEM] * 5,
        [((HEADS // 2, KEYS, 2 * READERS), f32, HBM)]
        + [((READERS, FEATURES + 2 * WIDTH), bf16, VMEM)] * SIDE,
        scratch=(pltpu.VMEM((HEADS // 2, KEYS, 2 * READERS), f32), sems((HEADS // 2,))),
        flops=5 * reader_product,
        moved=3 * megabyte,
    )(place, seen, rq, far_kv, keep, got)

    sums = []

    def segment_part(i):
        start, count = PARTS[i]
        dq, far, own = kernel_call(
            segment_kernel(start, count, i == 0),
            [SMEM] + [VMEM] * 4 + ([HBM, VMEM, VMEM] if sums else []),
            [
                ((ITEMS * HEADS, WIDTH), f32, HBM),
                ((KEYS, 2 * WIDTH), f32, VMEM),
                ((ITEMS, 2 * WIDTH), f32, VMEM),
            ],
            scratch=(
                pltpu.VMEM((KEYS + ITEMS, count), f32),
                pltpu.VMEM((KEYS + ITEMS, count), f32),
                pltpu.VMEM((count, WIDTH), f32),
                sems,
            ),
            aliases={5: 0, 6: 1, 7: 2} if sums else {},
            limit=24,
            flops=5 * 2 * (KEYS + ITEMS) * count * WIDTH,
            moved=4 * megabyte,
        )(place, q_rows, d_rows, far_kv, own_kv, *sums)
        sums[:] = [dq, far, own]

    q_rows, a[0] = together((q_rows, a[0]))
    a = [a[0]] + [shifted(a[i], "y", i) for i in range(1, SIDE)]
    segment_part(0)
    a, sums[:] = together((a, sums))

    *own, other, a_all, w_all = kernel_call(
        predict_kernel,
        [SMEM] + [VMEM] * 8,
        [((ROWS, WIDTH), f32, VMEM)] * SIDE
        + [
            ((SIDE, ROWS, WIDTH), bf16, VMEM),
            ((ROWS, FEATURES), bf16, HBM),
            ((SIDE, 2 * WIDTH, FEATURES), bf16, HBM),
        ],
        scratch=(
            pltpu.VMEM((ROWS, FEATURES), bf16),
            pltpu.VMEM((SIDE, 2 * WIDTH, FEATURES), bf16),
            sems((2,)),
        ),
        flops=product,
        moved=3 * megabyte,
    )(place, *a, *w)
    from_core = lax.ppermute(other, "core", CORES)
    base, *chip = kernel_call(
        chip_sum_kernel,
        [VMEM] * 5,
        [((ROWS, WIDTH), f32, VMEM)] + [((ROWS, WIDTH), bf16, VMEM)] * (SIDE - 1),
        moved=2 * megabyte,
    )(*own, from_core)
    q_rows, base = together((q_rows, base))
    arrived = [shifted(chip[i - 1], "z", i) for i in range(1, SIDE)]
    segment_part(1)
    arrived, sums[:] = together((arrived, sums))
    for part in arrived:
        base = base + part.astype(f32)
    error = base.astype(bf16)

    q_rows, error = together((q_rows, error))
    mine = [shifted(error, "z", i) for i in range(1, SIDE)]
    segment_part(2)
    mine, sums[:] = together((mine, sums))
    mine = [error] + mine
    others = [lax.ppermute(e, "core", CORES) for e in mine]
    stack = pltpu.VMEM((SIDE, ROWS, 2 * WIDTH), bf16)
    piece = (READERS, FEATURES)
    g = kernel_call(
        attended_grad_kernel,
        [SMEM] + [VMEM] * 8 + [HBM],
        [(piece, f32, VMEM)] + [(piece, bf16, VMEM)] * (SIDE - 1),
        scratch=(stack, pltpu.VMEM((SIDE, 2 * WIDTH, FEATURES), bf16), sems),
        flops=product,
        moved=3 * megabyte,
    )(place, *mine, *others, w_all)
    q_rows, mine[0], g_0 = together((q_rows, mine[0], g[0]))
    g = [g_0] + [shifted(g[i], "y", -i) for i in range(1, SIDE)]

    w_grad = kernel_call(
        projection_grad_kernel,
        [SMEM] + [VMEM] * 8 + [HBM],
        [((2 * WIDTH, FEATURES), f32, VMEM)] + [((2 * WIDTH, FEATURES), bf16, VMEM)] * (SIDE - 1),
        scratch=(stack, pltpu.VMEM((ROWS, FEATURES), bf16), sems),
        flops=product,
        moved=3 * megabyte,
    )(place, *mine, *others, a_all)
    segment_part(3)
    out_proj_grad = w_grad[0]
    for i in range(1, SIDE):
        out_proj_grad = out_proj_grad + shifted(w_grad[i], "x", i).astype(f32)

    q_items_grad, far_grad, own_grad = sums
    score_grad, beacon_grad = kernel_call(
        beacon_grad_kernel,
        [VMEM] * 4 + [HBM] + [VMEM] * 3,
        [((KEYS, HEADS * READERS), bf16, VMEM), ((KEYS, 2 * WIDTH), bf16, VMEM)],
        scratch=(pltpu.VMEM((HEADS // 2, KEYS, 2 * READERS), f32), sems((HEADS // 2,))),
        flops=4 * reader_product,
        moved=5 * megabyte,
    )(*g, probs, rq, far_kv, far_grad)

    pieces = beacon_grad.reshape(SEGMENTS, BEACONS, 2 * WIDTH)
    owned = lax.all_to_all(pieces, STRETCH, 0, 0, tiled=True)
    (reader_query_grad,) = kernel_call(
        query_grad_kernel,
        [VMEM] * 2,
        [((READERS, HEADS, WIDTH), f32, VMEM)],
        flops=reader_product,
        moved=2 * megabyte,
    )(score_grad, far_kv)
    k_items_grad, v_items_grad = kernel_call(
        items_grad_kernel,
        [VMEM] * 2,
        [((ITEMS, WIDTH), f32, VMEM)] * 2,
        moved=megabyte,
    )(own_grad, owned)
    q_items_grad = q_items_grad.reshape(1, ITEMS, HEADS, WIDTH)
    k_items_grad = k_items_grad.reshape(1, ITEMS, 1, WIDTH)
    v_items_grad = v_items_grad.reshape(1, ITEMS, 1, WIDTH)
    return q_items_grad, k_items_grad, v_items_grad, reader_query_grad, out_proj_grad


def solution(mesh):
    axes = Mesh(mesh.devices.reshape(SIDE, SIDE, SIDE, 2), STRETCH + HEAD)
    items = P(STRETCH, None, HEAD, None)
    return jax.shard_map(
        body,
        mesh=axes,
        in_specs=(
            items,
            items,
            items,
            items,
            P(STRETCH, HEAD, None),
            P(STRETCH),
            P(STRETCH, HEAD),
            P(STRETCH, HEAD),
        ),
        out_specs=(items, items, items, P(STRETCH, HEAD, None), P(STRETCH, HEAD)),
        check_vma=False,
    )
```
